32 devices in a mesh: parts: 2 (over y), mp: 4 (over z), shot: 4 (over x, core).
Axes of the slice: x: 2, y: 2, z: 4, core: 2. Of those that a mesh axis runs over, the one named last changes fastest.
Arguments:
- courant: float32 [192, 256, 128], P(('parts', 'mp')), parts along dimension 0, may hold values from 0.04 to 0.2
- forward_old: float32 [8, 96, 256, 128], P(('parts', 'shot'), 'mp'), parts along dimension 0, may hold values from -5 to 5
- forward_now: float32 [8, 96, 256, 128], P(('parts', 'shot'), 'mp'), parts along dimension 0, may hold values from -5 to 5
- adjoint_late: float32 [8, 96, 256, 128], P(('parts', 'shot'), 'mp'), parts along dimension 0, may hold values from -5 to 5
- adjoint_now: float32 [8, 96, 256, 128], P(('parts', 'shot'), 'mp'), parts along dimension 0, may hold values from -5 to 5
- src_cell: int32 [8, 64], P(('parts', 'shot')), parts along dimension 0, may hold values from 0 to 3145727
- src_sign: int32 [8, 64], P(('parts', 'shot')), parts along dimension 0, may hold values from 0 to 1
- wavelet: float32 [8, 2, 64], P(('parts', 'shot')), parts along dimension 0, may hold values from -16 to 16
- rec_cell: int32 [4096], P('parts'), parts along dimension 0, may hold values from 0 to 3145727
- rec_data: float32 [8, 2, 2048], P(('parts', 'shot')), parts along dimension 0, may hold values from -16 to 16
Outputs:
- raw_gradient: float32 [192, 256, 128], P(('parts', 'mp'), 'shot'), parts along dimension 0
- smooth_gradient: float32 [192, 256, 128], P(('parts', 'shot'), None, 'mp'), parts along dimension 0
The draws below stay inside these ranges and needn't reach their ends.
There are 2 independent parts, one for each index of `parts`. The reference program is written for one: setup_inputs(seed, part) draws one part's arguments, and reference() takes and returns one part's arrays. A program takes and returns all parts, laid end to end along the dimension named above; each array names one. Nothing has to cross between parts.
All inputs are finite; a program needn't handle non-finite values.
Results may differ from the reference program's by a relative error of at most 0.00025.
Values sent between devices are 32-bit elements; how exact they have to be, the bound alone decides.
A program may use at most 128 MiB of HBM per device.

```python
import math
import jax
import jax.numpy as jnp
from jax import lax

NY = 256
NZ = 128
NSRC = 64
NREC = 2048
SMOOTH_X = 32
SMOOTH_YZ = 4
NX = 96
SHOTS = 4


def set_ends(array, own_key, low, top_value):
    place = [jax.random.randint(jax.random.fold_in(own_key, axis), (), 0, length) for axis, length in enumerate(array.shape)]
    widest = array.shape.index(max(array.shape))
    next_to = place[:widest] + [(place[widest] + 1) % array.shape[widest]] + place[widest + 1:]
    return array.at[tuple(place)].set(low).at[tuple(next_to)].set(top_value)


def steps_of(rng, shape, split, low, high):
    level, own = 1.0, jax.random.fold_in(rng, 6)
    for dim, blocks in split:
        steps = jnp.exp(jax.random.uniform(jax.random.fold_in(own, dim), (blocks,), jnp.float32, low / len(split), high / len(split)))
        level = level * jnp.repeat(steps, shape[dim] // blocks).reshape([-1 if axis == dim else 1 for axis in range(len(shape))])
    return level


def normal_values(own_key, dims, spread, most, shards=(), held_as=jnp.bfloat16):
    entries = jax.random.normal(own_key, dims, jnp.float32) * spread
    if len(shards) > 0:
        entries = steps_of(own_key, dims, shards, -0.22, 0.18) * entries
    return jnp.clip(entries, min=-most, max=most).astype(held_as)


def setup_inputs(seed: int = 0, part: int = 0) -> dict:
    seeds = jax.random.split(jax.random.key(seed), 11)
    own_keys = jax.random.split(jax.random.fold_in(seeds[10], part), 11)
    return {
        "courant": jnp.clip(jnp.exp(math.log(0.2) - 1.609438 * jax.random.uniform(own_keys[0], (NX, NY, NZ), jnp.float32) ** steps_of(own_keys[0], (NX, NY, NZ), ((0, 4),), -0.2, 0.2)), 0.04, 0.2),
        "forward_old": normal_values(own_keys[1], (SHOTS, NX, NY, NZ), 0.7, 5.0, ((0, 4), (1, 4)), jnp.float32),
        "forward_now": normal_values(own_keys[2], (SHOTS, NX, NY, NZ), 0.7, 5.0, ((0, 4), (1, 4)), jnp.float32),
        "adjoint_late": normal_values(own_keys[3], (SHOTS, NX, NY, NZ), 0.7, 5.0, ((0, 4), (1, 4)), jnp.float32),
        "adjoint_now": normal_values(own_keys[4], (SHOTS, NX, NY, NZ), 0.7, 5.0, ((0, 4), (1, 4)), jnp.float32),
        "src_cell": set_ends(jax.random.randint(own_keys[5], (SHOTS, NSRC), 0, NX * NY * NZ), jax.random.fold_in(own_keys[5], 1), 0, (NX * NY * NZ) - 1).astype(jnp.int32),
        "src_sign": set_ends(jax.random.randint(own_keys[6], (SHOTS, NSRC), 0, 2), jax.random.fold_in(own_keys[6], 1), 0, 1).astype(jnp.int32),
        "wavelet": normal_values(own_keys[7], (SHOTS, 2, NSRC), 4.0, 16.0, ((0, 4),), jnp.float32),
        "rec_cell": set_ends(jax.random.randint(own_keys[8], (NREC,), 0, NX * NY * NZ), jax.random.fold_in(own_keys[8], 1), 0, (NX * NY * NZ) - 1).astype(jnp.int32),
        "rec_data": normal_values(own_keys[9], (SHOTS, 2, NREC), 4.0, 16.0, ((0, 4),), jnp.float32),
    }


COEFS = (8.0 / 5.0, -1.0 / 5.0, 8.0 / 315.0, -1.0 / 560.0)
CENTER = -205.0 / 72.0

def laplace(padded):
    row_count = padded.shape[-3] - 8
    center_rows = padded[..., 4:4 + row_count, :, :]
    leading = ((0, 0),) * (padded.ndim - 3)
    padded_yz = jnp.pad(center_rows, leading + ((0, 0), (4, 4), (4, 4)))
    width_y = center_rows.shape[-2]
    width_z = center_rows.shape[-1]
    accum_sum = 3.0 * CENTER * center_rows
    for offset, weight in enumerate(COEFS):
        reach = offset + 1
        along_x = padded[..., 4 + reach:4 + reach + row_count, :, :] + padded[..., 4 - reach:4 - reach + row_count, :, :]
        along_y = padded_yz[..., :, 4 + reach:4 + reach + width_y, 4:4 + width_z] + padded_yz[..., :, 4 - reach:4 - reach + width_y, 4:4 + width_z]
        along_z = padded_yz[..., :, 4:4 + width_y, 4 + reach:4 + reach + width_z] + padded_yz[..., :, 4:4 + width_y, 4 - reach:4 - reach + width_z]
        accum_sum = accum_sum + weight * (along_x + along_y + along_z)
    return accum_sum

def inject(field, cells, values, first_row):
    plane_size = field.shape[-2] * field.shape[-1]
    local_cell = cells - first_row * plane_size
    valid = (local_cell >= 0) & (local_cell < field.size)
    target = jnp.where(valid, local_cell, field.size)
    return field.reshape(-1).at[target].add(values, mode='drop').reshape(field.shape)

def sine_table(length):
    counter = jnp.arange(length, dtype=jnp.int32) + 1
    product = counter[:, None] * counter[None, :] % (2 * (length + 1))
    return jnp.sin(jnp.pi * product.astype(jnp.float32) / (length + 1))

def response(length, strength):
    counter = jnp.arange(length, dtype=jnp.int32) + 1
    half_sine = jnp.sin(jnp.pi * counter.astype(jnp.float32) / (2 * (length + 1)))
    return 1.0 / (1.0 + strength * 4.0 * half_sine * half_sine)

def spread_scale(fx_resp, fy_resp, fz_resp):
    return 1.0 / jnp.sqrt(jnp.mean(fx_resp * fx_resp)) * (1.0 / jnp.sqrt(jnp.mean(fy_resp * fy_resp))) * (1.0 / jnp.sqrt(jnp.mean(fz_resp * fz_resp)))

def pad_rows(field):
    return jnp.pad(field, ((4, 4), (0, 0), (0, 0)))

def reference(courant, forward_old, forward_now, adjoint_late, adjoint_now, src_cell, src_sign, wavelet, rec_cell, rec_data):
    total_sum = jnp.zeros(courant.shape, jnp.float32)
    for group in range(SHOTS):
        signed = (2 * src_sign[group] - 1).astype(jnp.float32)
        now_fwd = forward_now[group]
        now_adj = adjoint_now[group]
        accel_first = inject(courant * laplace(pad_rows(now_fwd)), src_cell[group], signed * wavelet[group, 0], 0)
        next_fwd = 2.0 * now_fwd - forward_old[group] + accel_first
        accel_second = inject(courant * laplace(pad_rows(next_fwd)), src_cell[group], signed * wavelet[group, 1], 0)
        mid_adj = 2.0 * now_adj - adjoint_late[group] + inject(courant * laplace(pad_rows(now_adj)), rec_cell, rec_data[group, 0], 0)
        first_adj = 2.0 * mid_adj - now_adj + inject(courant * laplace(pad_rows(mid_adj)), rec_cell, rec_data[group, 1], 0)
        total_sum = total_sum + (first_adj * accel_first + mid_adj * accel_second)
    raw_gradient = total_sum / SHOTS
    highest = lax.Precision.HIGHEST
    table_x = sine_table(NX)
    table_y = sine_table(NY)
    table_z = sine_table(NZ)
    fx_resp = response(NX, float(SMOOTH_X * SMOOTH_X))
    fy_resp = response(NY, float(SMOOTH_YZ * SMOOTH_YZ))
    fz_resp = response(NZ, float(SMOOTH_YZ * SMOOTH_YZ))
    spectrum = jnp.einsum('ia,abc->ibc', table_x, raw_gradient, precision=highest)
    spectrum = jnp.einsum('jb,ibc->ijc', table_y, spectrum, precision=highest)
    spectrum = jnp.einsum('kc,ijc->ijk', table_z, spectrum, precision=highest)
    spectrum = spectrum * (fx_resp[:, None, None] * fy_resp[None, :, None] * fz_resp[None, None, :])
    spectrum = jnp.einsum('ia,abc->ibc', table_x, spectrum, precision=highest)
    spectrum = jnp.einsum('jb,ibc->ijc', table_y, spectrum, precision=highest)
    spectrum = jnp.einsum('kc,ijc->ijk', table_z, spectrum, precision=highest)
    factor = 2.0 / (NX + 1) * (2.0 / (NY + 1)) * (2.0 / (NZ + 1))
    smooth_gradient = spectrum * (factor * spread_scale(fx_resp, fy_resp, fz_resp))
    return (raw_gradient, smooth_gradient)
```

```python
import functools
import math

import jax
import jax.numpy as jnp
import numpy as np
from jax import lax
from jax.experimental import pallas as pl
from jax.experimental.pallas import tpu as pltpu
from jax.sharding import PartitionSpec as P

SMOOTH_X = 32
SMOOTH_YZ = 4
COEFS = (8.0 / 5.0, -1.0 / 5.0, 8.0 / 315.0, -1.0 / 560.0)
CENTER = -205.0 / 72.0
REACH = 4
HIGHEST = lax.Precision.HIGHEST


def smoothing_table(length, strength):
    counter = np.arange(1, length + 1, dtype=np.float64)
    sines = np.sin(np.pi * np.outer(counter, counter) / (length + 1))
    half_sine = np.sin(np.pi * counter / (2 * (length + 1)))
    resp = 1.0 / (1.0 + strength * 4.0 * half_sine**2)
    table = 2.0 / (length + 1) * (sines * resp[None, :]) @ sines
    return table, 1.0 / math.sqrt(np.mean(resp * resp))


def stencil_table(length, center):
    table = np.eye(length) * center
    for offset, weight in enumerate(COEFS):
        reach = offset + 1
        if reach < length:
            table += weight * (np.eye(length, k=reach) + np.eye(length, k=-reach))
    return table


def split_table(table):
    high = jnp.asarray(table, jnp.float32).astype(jnp.bfloat16)
    rest = table - np.asarray(high.astype(jnp.float32), np.float64)
    return np.asarray(high), np.asarray(jnp.asarray(rest, jnp.float32).astype(jnp.bfloat16))


def stencil_tables(width_y, width_z):
    with jax.ensure_compile_time_eval():
        y_high, y_low = split_table(stencil_table(width_y, 3.0 * CENTER))
        z_high, z_low = split_table(np.kron(np.eye(2), stencil_table(width_z, 0.0)))
    table_y = np.concatenate([y_high, y_high, y_low], axis=1)
    table_z = np.concatenate([z_high, z_high, z_low], axis=0)
    return table_y, table_z


def scatter_kernel(
    rec_row, rec_lane, rec_first, rec_second, src_row, src_lane, src_first, src_second, *outs
):
    source_0, source_1, data_0, data_1 = outs
    zero = jnp.zeros(source_0.shape, jnp.float32)
    for out in outs:
        out[...] = zero
    lanes = lax.broadcasted_iota(jnp.int32, (1, source_0.shape[1]), 1)

    def add_all(rows, columns, first, second, out_first, out_second):
        count = rows.shape[0]
        unroll = math.gcd(count, 8)

        def some(step, carry):
            for extra in range(unroll):
                item = step * unroll + extra
                row = rows[item]
                hit = lanes == columns[item]
                out_first[pl.ds(row, 1), :] += jnp.where(hit, first[item], 0.0)
                out_second[pl.ds(row, 1), :] += jnp.where(hit, second[item], 0.0)
            return carry

        lax.fori_loop(0, count // unroll, some, 0)

    add_all(rec_row, rec_lane, rec_first, rec_second, data_0, data_1)
    add_all(src_row, src_lane, src_first, src_second, source_0, source_1)


def localize(cells, first, second, first_row, shape):
    size = shape[0] * shape[1] * shape[2]
    local = cells - first_row * shape[1] * shape[2]
    valid = (local >= 0) & (local < size)
    local = jnp.where(valid, local, 0)
    return (
        local // shape[2],
        local % shape[2],
        jnp.where(valid, first, 0.0),
        jnp.where(valid, second, 0.0),
    )


def injections(src, rec, shape):
    flat = jax.ShapeDtypeStruct((shape[0] * shape[1], shape[2]), jnp.float32)
    outs = pl.pallas_call(
        scatter_kernel,
        out_shape=(flat,) * 4,
        in_specs=[pl.BlockSpec(memory_space=pltpu.SMEM)] * 8,
        out_specs=(pl.BlockSpec(memory_space=pltpu.VMEM),) * 4,
        compiler_params=pltpu.CompilerParams(vmem_limit_bytes=24 * 2**20),
        cost_estimate=pl.CostEstimate(flops=0, bytes_accessed=50 * 2**20, transcendentals=0),
        name="inject",
    )(*rec, *src)
    return [out.reshape(shape) for out in outs]


def slab_laplace(row, window_f, window_a, table_y, table_z, low_mask, high_mask):
    field_f = window_f[1][row]
    field_a = window_a[1][row]
    both = jnp.concatenate([field_f, field_a], axis=1)
    high = both.astype(jnp.bfloat16)
    low = (both - high.astype(jnp.float32)).astype(jnp.bfloat16)
    total = jnp.dot(
        table_y[...],
        jnp.concatenate([high, low, high], axis=0),
        preferred_element_type=jnp.float32,
    ) + jnp.dot(
        jnp.concatenate([high, low, high], axis=1),
        table_z[...],
        preferred_element_type=jnp.float32,
    )
    width = field_f.shape[1]
    laps = []
    for window, part in ((window_f, total[:, :width]), (window_a, total[:, width:])):
        for offset, weight in enumerate(COEFS):
            reach = offset + 1
            down, up = row - reach, row + reach
            if down >= 0 and up < REACH:
                part = part + weight * (window[1][down] + window[1][up])
                continue
            part = part + (
                weight * window[1][down]
                if down >= 0
                else (weight * low_mask) * window[0][down + REACH]
            )
            part = part + (
                weight * window[1][up]
                if up < REACH
                else (weight * high_mask) * window[2][up - REACH]
            )
        laps.append(part)
    return laps


def edge_masks():
    step, count = pl.program_id(0), pl.num_programs(0)
    return (
        jnp.where(step > 0, 1.0, 0.0).astype(jnp.float32),
        jnp.where(step < count - 1, 1.0, 0.0).astype(jnp.float32),
    )


def first_kernel(
    f_before, f_now, f_after, a_before, a_now, a_after, courant, f_old, a_late, source, data,
    table_y, table_z, accel, f_next, a_mid,
):
    low_mask, high_mask = edge_masks()
    window_f, window_a = (f_before, f_now, f_after), (a_before, a_now, a_after)
    for row in range(REACH):
        lap_f, lap_a = slab_laplace(
            row, window_f, window_a, table_y, table_z, low_mask, high_mask
        )
        here = courant[row]
        accel_row = here * lap_f + source[row]
        accel[row] = accel_row
        f_next[row] = (2.0 * f_now[row] - f_old[row]) + accel_row
        a_mid[row] = (2.0 * a_now[row] - a_late[row]) + (here * lap_a + data[row])


def second_kernel(
    f_before, f_now, f_after, a_before, a_now, a_after, courant, a_old, accel, source, data,
    table_y, table_z, term,
):
    low_mask, high_mask = edge_masks()
    window_f, window_a = (f_before, f_now, f_after), (a_before, a_now, a_after)
    for row in range(REACH):
        lap_f, lap_a = slab_laplace(
            row, window_f, window_a, table_y, table_z, low_mask, high_mask
        )
        here = courant[row]
        accel_second = here * lap_f + source[row]
        a_row = a_now[row]
        a_first = (2.0 * a_row - a_old[row]) + (here * lap_a + data[row])
        term[row] = a_first * accel[row] + a_row * accel_second


def slab_step(kernel, outs, field_f, field_a, others, tables, name):
    rows, width_y, width_z = field_f.shape
    blocks = rows // REACH
    block = (REACH, width_y, width_z)
    here = pl.BlockSpec(block, lambda i: (i, 0, 0))
    before = pl.BlockSpec(block, lambda i: (jnp.maximum(i - 1, 0), 0, 0))
    after = pl.BlockSpec(block, lambda i: (jnp.minimum(i + 1, blocks - 1), 0, 0))
    whole = [pl.BlockSpec(table.shape, lambda i: (0, 0)) for table in tables]
    shape = jax.ShapeDtypeStruct(field_f.shape, jnp.float32)
    return pl.pallas_call(
        kernel,
        grid=(blocks,),
        out_shape=(shape,) * outs,
        in_specs=[before, here, after] * 2 + [here] * len(others) + whole,
        out_specs=(here,) * outs,
        compiler_params=pltpu.CompilerParams(
            dimension_semantics=("arbitrary",), vmem_limit_bytes=40 * 2**20
        ),
        cost_estimate=pl.CostEstimate(
            flops=2**33, bytes_accessed=40 * 2**20, transcendentals=0
        ),
        name=name,
    )(field_f, field_f, field_f, field_a, field_a, field_a, *others, *tables)


def halo_terms(side, row, halo, field):
    total = None
    for offset, weight in enumerate(COEFS):
        reach = offset + 1
        plane = row - reach + REACH if side == 0 else row + reach - REACH
        if 0 <= plane < REACH:
            part = weight * halo[field, plane]
            total = part if total is None else total + part
    return total


def first_edge_kernel(
    halo_low, halo_high, courant, accel_in, next_in, mid_in, accel, f_next, a_mid, low, high
):
    for side, halo, edge in ((0, halo_low, low), (1, halo_high, high)):

        @pl.when(pl.program_id(0) == side)
        def _():
            for row in range(REACH):
                here = courant[row]
                add_f = here * halo_terms(side, row, halo, 0)
                add_a = here * halo_terms(side, row, halo, 1)
                accel[row] = accel_in[row] + add_f
                next_row = next_in[row] + add_f
                mid_row = mid_in[row] + add_a
                f_next[row] = next_row
                a_mid[row] = mid_row
                edge[0, row] = next_row
                edge[1, row] = mid_row


def second_edge_kernel(halo_low, halo_high, courant, accel, a_mid, term, edge):
    for side, halo in ((0, halo_low), (1, halo_high)):

        @pl.when(pl.program_id(0) == side)
        def _():
            for row in range(REACH):
                here = courant[row]
                add_f = here * halo_terms(side, row, halo, 0)
                add_a = here * halo_terms(side, row, halo, 1)
                edge[row] = term[row] + (add_a * accel[row] + a_mid[row] * add_f)


def edge_specs(shape):
    last = shape[0] // REACH - 1
    block = (REACH,) + shape[1:]
    both = pl.BlockSpec((2,) + block, lambda i: (0, 0, 0, 0))
    edge = pl.BlockSpec(block, lambda i: (i * last, 0, 0))
    side = pl.BlockSpec(block, lambda i: (i, 0, 0))
    return both, edge, side


EDGE_PARAMS = dict(dimension_semantics=("arbitrary",), vmem_limit_bytes=32 * 2**20)


def first_edges(low, high, courant, accel, f_next, a_mid):
    both, edge, _ = edge_specs(courant.shape)
    full = jax.ShapeDtypeStruct(courant.shape, jnp.float32)
    pair = jax.ShapeDtypeStruct(low.shape, jnp.float32)
    return pl.pallas_call(
        first_edge_kernel,
        grid=(2,),
        out_shape=(full, full, full, pair, pair),
        in_specs=[both, both, edge, edge, edge, edge],
        out_specs=(edge, edge, edge, both, both),
        input_output_aliases={3: 0, 4: 1, 5: 2},
        compiler_params=pltpu.CompilerParams(**EDGE_PARAMS),
        name="first_edges",
    )(low, high, courant, accel, f_next, a_mid)


def second_edges(low, high, courant, accel, a_mid, term):
    both, edge, side = edge_specs(courant.shape)
    shape = jax.ShapeDtypeStruct((2 * REACH,) + courant.shape[1:], jnp.float32)
    return pl.pallas_call(
        second_edge_kernel,
        grid=(2,),
        out_shape=shape,
        in_specs=[both, both, edge, edge, edge, edge],
        out_specs=side,
        compiler_params=pltpu.CompilerParams(**EDGE_PARAMS),
        name="second_edges",
    )(low, high, courant, accel, a_mid, term)


def exchange(low_edge, high_edge):
    count = lax.axis_size("mp")
    upward = [(i, i + 1) for i in range(count - 1)]
    downward = [(i + 1, i) for i in range(count - 1)]
    return lax.ppermute(high_edge, "mp", upward), lax.ppermute(low_edge, "mp", downward)


def sum_groups(term):
    count = lax.axis_size("shot")
    place = lax.axis_index("shot")
    rows, width_y, width_z = term.shape
    part = term.reshape(rows, count, width_y // count, width_z)
    bit = 1
    while bit < count:
        split = part.reshape(rows, part.shape[1] // 2, 2, part.shape[2], width_z)
        own = (place // bit) % 2
        mine = lax.dynamic_index_in_dim(split, own, 2, keepdims=False)
        other = lax.dynamic_index_in_dim(split, 1 - own, 2, keepdims=False)
        part = mine + lax.ppermute(other, "shot", [(i, i ^ bit) for i in range(count)])
        bit *= 2
    return part[:, 0]


def per_device(
    courant,
    forward_old,
    forward_now,
    adjoint_late,
    adjoint_now,
    src_cell,
    src_sign,
    wavelet,
    rec_cell,
    rec_data,
):
    shape = courant.shape
    slab_rows = shape[0]
    first_row = lax.axis_index("mp") * slab_rows
    old_fwd, now_fwd = forward_old[0], forward_now[0]
    late_adj, now_adj = adjoint_late[0], adjoint_now[0]
    tables = [jnp.asarray(table) for table in stencil_tables(shape[1], shape[2])]

    halo_low, halo_high = exchange(
        jnp.stack([now_fwd[:REACH], now_adj[:REACH]]),
        jnp.stack([now_fwd[-REACH:], now_adj[-REACH:]]),
    )
    signed = (2 * src_sign[0] - 1).astype(jnp.float32)
    src = localize(src_cell[0], signed * wavelet[0, 0], signed * wavelet[0, 1], first_row, shape)
    rec = localize(rec_cell, rec_data[0, 0], rec_data[0, 1], first_row, shape)
    source_0, source_1, data_0, data_1 = injections(src, rec, shape)
    accel, next_fwd, mid_adj = slab_step(
        first_kernel, 3, now_fwd, now_adj,
        (courant, old_fwd, late_adj, source_0, data_0), tables, "first_step",
    )
    accel, next_fwd, mid_adj, low_edge, high_edge = first_edges(
        halo_low, halo_high, courant, accel, next_fwd, mid_adj
    )
    halo_low, halo_high = exchange(low_edge, high_edge)
    (term,) = slab_step(
        second_kernel, 1, next_fwd, mid_adj,
        (courant, now_adj, accel, source_1, data_1), tables, "second_step",
    )
    inner = sum_groups(term[REACH:-REACH])
    outer = sum_groups(second_edges(halo_low, halo_high, courant, accel, mid_adj, term))
    summed = jnp.concatenate([outer[:REACH], inner, outer[REACH:]], axis=0)
    raw_gradient = summed / lax.axis_size("shot")

    table_x, spread_x = smoothing_table(slab_rows * lax.axis_size("mp"), SMOOTH_X**2)
    table_y, spread_y = smoothing_table(shape[1], SMOOTH_YZ**2)
    table_z, spread_z = smoothing_table(shape[2], SMOOTH_YZ**2)
    table_y = table_y * (spread_x * spread_y * spread_z)
    table_x, table_y, table_z = (
        jnp.asarray(table, jnp.float32) for table in (table_x, table_y, table_z)
    )
    depth_done = jnp.einsum("abk,jk->abj", raw_gradient, table_z, precision=HIGHEST)
    x_done = jnp.einsum(
        "ia,abc->ibc",
        table_x,
        lax.all_to_all(depth_done, "mp", split_axis=2, concat_axis=0, tiled=True),
        precision=HIGHEST,
    )
    smooth_gradient = jnp.einsum(
        "jb,abc->ajc",
        table_y,
        lax.all_to_all(x_done, "shot", split_axis=0, concat_axis=1, tiled=True),
        precision=HIGHEST,
    )
    return (raw_gradient, smooth_gradient)


def solution(mesh):
    return jax.shard_map(
        per_device,
        mesh=mesh,
        in_specs=(
            P(("parts", "mp"), None, None),
            P(("parts", "shot"), "mp", None, None),
            P(("parts", "shot"), "mp", None, None),
            P(("parts", "shot"), "mp", None, None),
            P(("parts", "shot"), "mp", None, None),
            P(("parts", "shot"), None),
            P(("parts", "shot"), None),
            P(("parts", "shot"), None, None),
            P("parts"),
            P(("parts", "shot"), None, None),
        ),
        out_specs=(P(("parts", "mp"), "shot", None), P(("parts", "shot"), None, "mp")),
        check_vma=False,
    )
```

```python
import functools
import math

import jax
import jax.numpy as jnp
import numpy as np
from jax import lax
from jax.experimental import pallas as pl
from jax.experimental.pallas import tpu as pltpu
from jax.sharding import PartitionSpec as P

SMOOTH_X = 32
SMOOTH_YZ = 4
COEFS = (8.0 / 5.0, -1.0 / 5.0, 8.0 / 315.0, -1.0 / 560.0)
CENTER = -205.0 / 72.0
REACH = 4
HIGHEST = lax.Precision.HIGHEST

VMEM_GRANT = 60 * 2**20


def smoothing_table(length, strength):
    counter = np.arange(1, length + 1, dtype=np.float64)
    sines = np.sin(np.pi * np.outer(counter, counter) / (length + 1))
    half_sine = np.sin(np.pi * counter / (2 * (length + 1)))
    resp = 1.0 / (1.0 + strength * 4.0 * half_sine**2)
    table = 2.0 / (length + 1) * (sines * resp[None, :]) @ sines
    return table, 1.0 / math.sqrt(np.mean(resp * resp))


def stencil_table(length, center):
    table = np.eye(length) * center
    for offset, weight in enumerate(COEFS):
        reach = offset + 1
        if reach < length:
            table += weight * (np.eye(length, k=reach) + np.eye(length, k=-reach))
    return table


def split_table(table):
    high = jnp.asarray(table, jnp.float32).astype(jnp.bfloat16)
    rest = table - np.asarray(high.astype(jnp.float32), np.float64)
    return np.asarray(high), np.asarray(jnp.asarray(rest, jnp.float32).astype(jnp.bfloat16))


def stencil_tables(width_y, width_z):
    with jax.ensure_compile_time_eval():
        y_high, y_low = split_table(stencil_table(width_y, 3.0 * CENTER))
        z_high, z_low = split_table(np.kron(np.eye(2), stencil_table(width_z, 0.0)))
    table_y = np.concatenate([y_high, y_high, y_low], axis=1)
    table_z = np.concatenate([z_high, z_high, z_low], axis=0)
    return table_y, table_z


def scatter_kernel(
    rec_cell, rec_first, rec_second, src_cell, src_first, src_second, base, *outs
):
    *outs, rec_list, src_list = outs
    source_0, source_1, data_0, data_1 = outs
    rows, width = source_0.shape
    zero = jnp.zeros(source_0.shape, jnp.float32)
    for out in outs:
        out[...] = zero
    lanes = lax.broadcasted_iota(jnp.int32, (1, width), 1)
    first_cell = base[0]

    def add_all(cells, first, second, found, out_first, out_second):
        count = cells.shape[0]
        unroll = math.gcd(count, 16)

        def keep(step, kept):
            for extra in range(unroll):
                item = step * unroll + extra
                local = cells[item] - first_cell
                found[kept] = item
                kept += jnp.where((local >= 0) & (local < rows * width), 1, 0)
            return kept

        kept = lax.fori_loop(0, count // unroll, keep, 0)

        def add_one(step, carry):
            item = found[step]
            local = cells[item] - first_cell
            row = local // width
            hit = lanes == local - row * width
            out_first[pl.ds(row, 1), :] += jnp.where(hit, first[item], 0.0)
            out_second[pl.ds(row, 1), :] += jnp.where(hit, second[item], 0.0)
            return carry

        lax.fori_loop(0, kept, add_one, 0)

    add_all(rec_cell, rec_first, rec_second, rec_list, data_0, data_1)
    add_all(src_cell, src_first, src_second, src_list, source_0, source_1)


def injections(src, rec, first_cell, shape):
    flat = jax.ShapeDtypeStruct((shape[0] * shape[1], shape[2]), jnp.float32)
    outs = pl.pallas_call(
        scatter_kernel,
        out_shape=(flat,) * 4,
        in_specs=[pl.BlockSpec(memory_space=pltpu.SMEM)] * 7,
        out_specs=(pl.BlockSpec(memory_space=pltpu.VMEM),) * 4,
        scratch_shapes=[
            pltpu.SMEM((rec[0].shape[0] + 16,), jnp.int32),
            pltpu.SMEM((src[0].shape[0] + 16,), jnp.int32),
        ],
        compiler_params=pltpu.CompilerParams(vmem_limit_bytes=VMEM_GRANT),
        cost_estimate=pl.CostEstimate(flops=0, bytes_accessed=40 * 2**20, transcendentals=0),
        name="inject",
    )(*rec, *src, first_cell)
    return [out.reshape(shape) for out in outs]


def slab_laplace(place, fields, table_y, table_z):
    count = fields[0].shape[0]
    both = jnp.concatenate([field[place] for field in fields], axis=1)
    high = both.astype(jnp.bfloat16)
    low = (both - high.astype(jnp.float32)).astype(jnp.bfloat16)
    total = jnp.dot(
        table_y[...],
        jnp.concatenate([high, low, high], axis=0),
        preferred_element_type=jnp.float32,
    ) + jnp.dot(
        jnp.concatenate([high, low, high], axis=1),
        table_z[...],
        preferred_element_type=jnp.float32,
    )
    width = fields[0].shape[2]
    laps = [total[:, side * width : (side + 1) * width] for side in range(2)]
    for offset, weight in enumerate(COEFS):
        for shift in (offset + 1, -(offset + 1)):
            other = place + shift
            inside = (other >= 0) & (other < count)
            factor = jnp.where(inside, weight, 0.0).astype(jnp.float32)
            other = jnp.clip(other, 0, count - 1)
            laps = [lap + factor * field[other] for lap, field in zip(laps, fields)]
    return laps


def first_kernel(
    f_now, a_now, courant, f_old, a_late, source, data, table_y, table_z, accel, f_next, a_mid
):
    for row in range(REACH):
        place = pl.program_id(0) * REACH + row
        lap_f, lap_a = slab_laplace(place, (f_now, a_now), table_y, table_z)
        here = courant[row]
        accel_row = here * lap_f + source[row]
        accel[row] = accel_row
        f_next[row] = (2.0 * f_now[place] - f_old[row]) + accel_row
        a_mid[row] = (2.0 * a_now[place] - a_late[row]) + (here * lap_a + data[row])


def second_kernel(
    f_now, a_now, courant, a_old, accel, source, data, table_y, table_z, term
):
    for row in range(REACH):
        place = pl.program_id(0) * REACH + row
        lap_f, lap_a = slab_laplace(place, (f_now, a_now), table_y, table_z)
        here = courant[row]
        accel_second = here * lap_f + source[row]
        a_row = a_now[place]
        a_first = (2.0 * a_row - a_old[row]) + (here * lap_a + data[row])
        term[row] = a_first * accel[row] + a_row * accel_second


def slab_step(kernel, outs, field_f, field_a, others, tables):
    rows, width_y, width_z = field_f.shape
    blocks = rows // REACH
    block = (REACH, width_y, width_z)
    here = pl.BlockSpec(block, lambda i: (i, 0, 0))
    field = pl.BlockSpec(field_f.shape, lambda i: (0, 0, 0))
    whole = [pl.BlockSpec(table.shape, lambda i: (0, 0)) for table in tables]
    shape = jax.ShapeDtypeStruct(field_f.shape, jnp.float32)
    return pl.pallas_call(
        kernel,
        grid=(blocks,),
        out_shape=(shape,) * outs,
        in_specs=[field] * 2 + [here] * len(others) + whole,
        out_specs=(here,) * outs,
        compiler_params=pltpu.CompilerParams(
            dimension_semantics=("arbitrary",), vmem_limit_bytes=VMEM_GRANT
        ),
        cost_estimate=pl.CostEstimate(
            flops=2**33, bytes_accessed=40 * 2**20, transcendentals=0
        ),
    )(field_f, field_a, *others, *tables)


def halo_terms(side, row, halo, field):
    total = None
    for offset, weight in enumerate(COEFS):
        reach = offset + 1
        plane = row - reach + REACH if side == 0 else row + reach - REACH
        if 0 <= plane < REACH:
            part = weight * halo[field, plane]
            total = part if total is None else total + part
    return total


def first_edge_kernel(
    halo_low, halo_high, courant, accel_in, next_in, mid_in, accel, f_next, a_mid, low, high
):
    for side, halo, edge in ((0, halo_low, low), (1, halo_high, high)):

        @pl.when(pl.program_id(0) == side)
        def _():
            for row in range(REACH):
                here = courant[row]
                add_f = here * halo_terms(side, row, halo, 0)
                add_a = here * halo_terms(side, row, halo, 1)
                accel[row] = accel_in[row] + add_f
                next_row = next_in[row] + add_f
                mid_row = mid_in[row] + add_a
                f_next[row] = next_row
                a_mid[row] = mid_row
                edge[0, row] = next_row
                edge[1, row] = mid_row


def second_edge_kernel(halo_low, halo_high, courant, accel, a_mid, term, edge):
    for side, halo in ((0, halo_low), (1, halo_high)):

        @pl.when(pl.program_id(0) == side)
        def _():
            for row in range(REACH):
                here = courant[row]
                add_f = here * halo_terms(side, row, halo, 0)
                add_a = here * halo_terms(side, row, halo, 1)
                edge[row] = term[row] + (add_a * accel[row] + a_mid[row] * add_f)


def edge_specs(shape):
    last = shape[0] // REACH - 1
    block = (REACH,) + shape[1:]
    both = pl.BlockSpec((2,) + block, lambda i: (0, 0, 0, 0))
    edge = pl.BlockSpec(block, lambda i: (i * last, 0, 0))
    side = pl.BlockSpec(block, lambda i: (i, 0, 0))
    return both, edge, side


EDGE_PARAMS = dict(dimension_semantics=("arbitrary",), vmem_limit_bytes=VMEM_GRANT)


def first_edges(low, high, courant, accel, f_next, a_mid):
    both, edge, _ = edge_specs(courant.shape)
    full = jax.ShapeDtypeStruct(courant.shape, jnp.float32)
    pair = jax.ShapeDtypeStruct(low.shape, jnp.float32)
    return pl.pallas_call(
        first_edge_kernel,
        grid=(2,),
        out_shape=(full, full, full, pair, pair),
        in_specs=[both, both, edge, edge, edge, edge],
        out_specs=(edge, edge, edge, both, both),
        input_output_aliases={3: 0, 4: 1, 5: 2},
        compiler_params=pltpu.CompilerParams(**EDGE_PARAMS),
        name="first_edges",
    )(low, high, courant, accel, f_next, a_mid)


def second_edges(low, high, courant, accel, a_mid, term):
    both, edge, side = edge_specs(courant.shape)
    shape = jax.ShapeDtypeStruct((2 * REACH,) + courant.shape[1:], jnp.float32)
    return pl.pallas_call(
        second_edge_kernel,
        grid=(2,),
        out_shape=shape,
        in_specs=[both, both, edge, edge, edge, edge],
        out_specs=side,
        compiler_params=pltpu.CompilerParams(**EDGE_PARAMS),
        name="second_edges",
    )(low, high, courant, accel, a_mid, term)


def pack_kernel(f_low, f_high, a_low, a_high, low, high):
    low[0], low[1] = f_low[...], a_low[...]
    high[0], high[1] = f_high[...], a_high[...]


def pack_edges(field_f, field_a):
    block = (REACH,) + field_f.shape[1:]
    last = field_f.shape[0] // REACH - 1
    low = pl.BlockSpec(block, lambda i: (0, 0, 0))
    high = pl.BlockSpec(block, lambda i: (last, 0, 0))
    both = pl.BlockSpec((2,) + block, lambda i: (0, 0, 0, 0))
    pair = jax.ShapeDtypeStruct((2,) + block, jnp.float32)
    return pl.pallas_call(
        pack_kernel,
        grid=(1,),
        out_shape=(pair, pair),
        in_specs=[low, high, low, high],
        out_specs=(both, both),
        compiler_params=pltpu.CompilerParams(vmem_limit_bytes=VMEM_GRANT),
        name="pack_edges",
    )(field_f, field_f, field_a, field_a)


def exchange(low_edge, high_edge):
    count = lax.axis_size("mp")
    upward = [(i, i + 1) for i in range(count - 1)]
    downward = [(i + 1, i) for i in range(count - 1)]
    from_low = lax.ppermute(high_edge, "mp", upward)
    from_high = lax.ppermute(low_edge, "mp", downward)
    return from_low, from_high


def sum_groups(term):
    count = lax.axis_size("shot")
    place = lax.axis_index("shot")
    rows, width_y, width_z = term.shape
    part = term.reshape(rows, count, width_y // count, width_z)
    bit = 1
    while bit < count:
        split = part.reshape(rows, part.shape[1] // 2, 2, part.shape[2], width_z)
        own = (place // bit) % 2
        mine = lax.dynamic_index_in_dim(split, own, 2, keepdims=False)
        other = lax.dynamic_index_in_dim(split, 1 - own, 2, keepdims=False)
        sent = lax.ppermute(other, "shot", [(i, i ^ bit) for i in range(count)])
        part = mine + sent
        bit *= 2
    return part[:, 0]


def slab_tables(table, count):
    rows = table.shape[0] // count
    local, sums, gains = [], [], []
    for me in range(count):
        own = slice(me * rows, (me + 1) * rows)
        local.append(table[own, own])
        sums.append(np.stack([table[me * rows, own], table[(me + 1) * rows - 1, own]]))
        gain = []
        for shift in range(1, count):
            source = (me - shift) % count
            seen = (source + 1) * rows - 1 if source < me else source * rows
            gain.append(table[own, seen] / table[seen, seen])
        gains.append(np.stack(gain, axis=1) if gain else np.zeros((rows, 0)))
    mix = np.concatenate([np.stack(local), np.stack(gains)], axis=2)
    return mix.astype(np.float32), np.stack(sums).astype(np.float32)


def mean_kernel(groups, inner, outer, sums, raw, planes):
    rows, edge = raw.shape[0], outer.shape[0] // 2
    total = [None, None]
    for row in range(rows):
        if row < edge:
            plane = outer[row]
        elif row < rows - edge:
            plane = inner[row - edge]
        else:
            plane = outer[row - rows + 2 * edge]
        plane = plane / groups
        raw[row] = plane
        for side in range(2):
            part = sums[side, row] * plane
            total[side] = part if row == 0 else total[side] + part
    planes[0], planes[1] = total


def make_smooth_kernel(count, group, lines):
    def kernel(raw, *refs):
        planes, (mix, table_z) = refs[: count - 1], refs[count - 1 : count + 1]
        pieces, mixed = refs[count + 1 : -1], refs[-1]
        rows = raw.shape[0]
        step = math.gcd(rows, 4)

        def some(index, carry):
            base = index * step
            sums = [None] * step
            for source in range(rows + count - 1):
                plane = raw[source] if source < rows else planes[source - rows][0]
                for extra in range(step):
                    part = mix[base + extra, source] * plane
                    sums[extra] = part if source == 0 else sums[extra] + part
            for extra in range(step):
                mixed[base + extra] = sums[extra]
            return carry

        lax.fori_loop(0, rows // step, some, 0)
        apart = rows // group
        for place in range(apart):
            stacked = jnp.concatenate(
                [mixed[part * apart + place] for part in range(group)], axis=0
            )
            turned = lax.dot_general(
                table_z[...],
                stacked,
                (((1,), (1,)), ((), ())),
                precision=HIGHEST,
                preferred_element_type=jnp.float32,
            )
            for target, piece in enumerate(pieces):
                piece[place] = turned[target * lines : (target + 1) * lines]

    return kernel


def make_last_kernel(count, group, ratio):
    def kernel(*refs):
        pieces, table, out = refs[:count], refs[count], refs[count + 1]
        apart, lines, lanes = pieces[0].shape
        width = out.shape[2]
        whole = jnp.concatenate(
            [piece[...].reshape(apart * lines, lanes) for piece in pieces], axis=1
        )
        done = jnp.dot(whole, table[...], precision=HIGHEST, preferred_element_type=jnp.float32)
        for block in range(ratio * group):
            out[block * apart : (block + 1) * apart] = done[
                :, block * width : (block + 1) * width
            ].reshape(apart, lines, width)

    return kernel


VMEM = pl.BlockSpec(memory_space=pltpu.VMEM)
SMEM = pl.BlockSpec(memory_space=pltpu.SMEM)
GRANT = pltpu.CompilerParams(vmem_limit_bytes=VMEM_GRANT)


def smooth(inner, outer, slab_rows, width_y, width_z):
    slabs, groups = lax.axis_size("mp"), lax.axis_size("shot")
    slab, place = lax.axis_index("mp"), lax.axis_index("shot")
    ratio = slabs // groups
    lines_y, lines_z = width_y // groups, width_z // slabs
    group = max(1, 128 // lines_y)

    table_x, spread_x = smoothing_table(slab_rows * slabs, SMOOTH_X**2)
    table_y, spread_y = smoothing_table(width_y, SMOOTH_YZ**2)
    table_z, spread_z = smoothing_table(width_z, SMOOTH_YZ**2)
    table_y = table_y * (spread_x * spread_y * spread_z)
    mix, sums = (
        lax.dynamic_index_in_dim(jnp.asarray(table), slab, 0, keepdims=False)
        for table in slab_tables(table_x, slabs)
    )
    first = lax.rem(lax.rem(slab, ratio) * groups + place, slabs)
    table_z = jnp.asarray(np.concatenate([table_z, table_z]).astype(np.float32))
    table_z = lax.dynamic_slice_in_dim(table_z, first * lines_z, width_z, 0)
    last = np.zeros((slabs, group * lines_y, ratio * group, width_y))
    for number in range(slabs):
        lines = table_y[(number % groups) * lines_y :][:lines_y]
        for part in range(group):
            last[number, part * lines_y : (part + 1) * lines_y][
                :, (number // groups) * group + part
            ] = lines
    last = last.reshape(slabs, group * lines_y, -1)
    last = last[(-np.arange(slabs)) % slabs].astype(np.float32)
    last = lax.dynamic_slice_in_dim(
        jnp.asarray(np.concatenate([last, last])), lax.rem(slabs - slab, slabs), slabs, 0
    ).reshape(slabs * group * lines_y, -1)

    block = jax.ShapeDtypeStruct((slab_rows, lines_y, width_z), jnp.float32)
    raw, planes = pl.pallas_call(
        functools.partial(mean_kernel, float(groups)),
        out_shape=(block, jax.ShapeDtypeStruct((2, lines_y, width_z), jnp.float32)),
        in_specs=[VMEM, VMEM, SMEM],
        out_specs=(VMEM, VMEM),
        compiler_params=GRANT,
        name="mean",
    )(inner, outer, sums)
    received = []
    for shift in range(1, slabs):
        upward = jnp.where(slab + shift < slabs, 1, 0)
        sent = lax.dynamic_slice_in_dim(planes, upward, 1, 0)
        ring = [(i, (i + shift) % slabs) for i in range(slabs)]
        received.append(lax.ppermute(sent, "mp", ring))
    piece = jax.ShapeDtypeStruct((slab_rows // group, lines_z, group * lines_y), jnp.float32)
    pieces = pl.pallas_call(
        make_smooth_kernel(slabs, group, lines_z),
        out_shape=(piece,) * slabs,
        in_specs=[VMEM] * slabs + [SMEM, VMEM],
        out_specs=(VMEM,) * slabs,
        scratch_shapes=[pltpu.VMEM((slab_rows, lines_y, width_z), jnp.float32)],
        compiler_params=GRANT,
        name="smooth_xz",
    )(raw, *received, mix, table_z)
    arrived = []
    for shift, sent in enumerate(pieces):
        pairs = []
        for m in range(slabs):
            for s in range(groups):
                target = ((m % ratio) * groups + s + shift) % slabs
                pairs.append((m * groups + s, target * groups + m // ratio))
        arrived.append(lax.ppermute(sent, ("mp", "shot"), pairs))
    done = pl.pallas_call(
        make_last_kernel(slabs, group, ratio),
        out_shape=jax.ShapeDtypeStruct((slab_rows * ratio, lines_z, width_y), jnp.float32),
        in_specs=[VMEM] * (slabs + 1),
        out_specs=VMEM,
        compiler_params=GRANT,
        name="smooth_y",
    )(*arrived, last)
    return raw, jnp.swapaxes(done, 1, 2)


def one_device(
    courant,
    forward_old,
    forward_now,
    adjoint_late,
    adjoint_now,
    src_cell,
    src_sign,
    wavelet,
    rec_cell,
    rec_data,
):
    shape = courant.shape
    slab_rows = shape[0]
    first_row = lax.axis_index("mp") * slab_rows
    old_fwd, now_fwd = forward_old[0], forward_now[0]
    late_adj, now_adj = adjoint_late[0], adjoint_now[0]
    tables = [jnp.asarray(table) for table in stencil_tables(shape[1], shape[2])]

    signed = (2 * src_sign[0] - 1).astype(jnp.float32)
    halo_low, halo_high = exchange(*pack_edges(now_fwd, now_adj))
    first_cell = (first_row * shape[1] * shape[2]).astype(jnp.int32).reshape(1)
    source_0, source_1, data_0, data_1 = injections(
        (src_cell[0], signed * wavelet[0, 0], signed * wavelet[0, 1]),
        (rec_cell, rec_data[0, 0], rec_data[0, 1]),
        first_cell,
        shape,
    )
    accel, next_fwd, mid_adj = slab_step(
        first_kernel, 3, now_fwd, now_adj,
        (courant, old_fwd, late_adj, source_0, data_0), tables,
    )
    accel, next_fwd, mid_adj, low_edge, high_edge = first_edges(
        halo_low, halo_high, courant, accel, next_fwd, mid_adj
    )
    halo_low, halo_high = exchange(low_edge, high_edge)
    (term,) = slab_step(
        second_kernel, 1, next_fwd, mid_adj,
        (courant, now_adj, accel, source_1, data_1), tables,
    )
    inner = sum_groups(term[REACH:-REACH])
    outer = sum_groups(second_edges(halo_low, halo_high, courant, accel, mid_adj, term))
    return smooth(inner, outer, shape[0], shape[1], shape[2])


def solution(mesh):
    return jax.shard_map(
        one_device,
        mesh=mesh,
        in_specs=(
            P(("parts", "mp"), None, None),
            P(("parts", "shot"), "mp", None, None),
            P(("parts", "shot"), "mp", None, None),
            P(("parts", "shot"), "mp", None, None),
            P(("parts", "shot"), "mp", None, None),
            P(("parts", "shot"), None),
            P(("parts", "shot"), None),
            P(("parts", "shot"), None, None),
            P("parts"),
            P(("parts", "shot"), None, None),
        ),
        out_specs=(P(("parts", "mp"), "shot", None), P(("parts", "shot"), None, "mp")),
        check_vma=False,
    )
```

```python
import functools
import math

import jax
import jax.numpy as jnp
import numpy as np
from jax import lax
from jax.experimental import pallas as pl
from jax.experimental.pallas import tpu as pltpu
from jax.sharding import PartitionSpec as P

SMOOTH_X = 32
SMOOTH_YZ = 4
COEFS = (8.0 / 5.0, -1.0 / 5.0, 8.0 / 315.0, -1.0 / 560.0)
CENTER = -205.0 / 72.0
REACH = 4
HIGHEST = lax.Precision.HIGHEST

VMEM_GRANT = 60 * 2**20


def smoothing_table(length, strength):
    counter = np.arange(1, length + 1, dtype=np.float64)
    sines = np.sin(np.pi * np.outer(counter, counter) / (length + 1))
    half_sine = np.sin(np.pi * counter / (2 * (length + 1)))
    resp = 1.0 / (1.0 + strength * 4.0 * half_sine**2)
    table = 2.0 / (length + 1) * (sines * resp[None, :]) @ sines
    return table, 1.0 / math.sqrt(np.mean(resp * resp))


SCALE = 5040.0
WHOLE = tuple(float(round(SCALE * weight)) for weight in COEFS)
MIDDLE = 3.0 * float(round(SCALE * CENTER))


def stencil_tables(width_y, width_z):
    def bands(length):
        return sum(
            weight * (np.eye(length, k=offset + 1) + np.eye(length, k=-offset - 1))
            for offset, weight in enumerate(WHOLE)
        )

    band_y = bands(width_y)
    band_z = np.kron(np.eye(2), bands(width_z))
    return (
        jnp.asarray(np.concatenate([band_y, band_y], axis=1), jnp.bfloat16),
        jnp.asarray(np.concatenate([band_z, band_z], axis=0), jnp.bfloat16),
    )


def scatter_kernel(
    rec_row, rec_lane, rec_first, rec_second, src_row, src_lane, src_first, src_second, *outs
):
    source_0, source_1, data_0, data_1 = outs
    zero = jnp.zeros(source_0.shape, jnp.float32)
    for out in outs:
        out[...] = zero
    lanes = lax.broadcasted_iota(jnp.int32, (1, source_0.shape[1]), 1)

    def add_all(rows, columns, first, second, targets):
        count = rows.shape[0]
        group = math.gcd(count, 4)

        def some(step, carry):
            items = [step * group + extra for extra in range(group)]
            places = [rows[item] for item in items]
            hits = [lanes == columns[item] for item in items]
            for values, out in zip((first, second), targets):
                added = [jnp.where(hit, values[item], 0.0) for hit, item in zip(hits, items)]
                sums = []
                for late in range(group):
                    total = added[late]
                    for early in range(late):
                        total += jnp.where(places[early] == places[late], added[early], 0.0)
                    sums.append(out[pl.ds(places[late], 1), :] + total)
                for place, total in zip(places, sums):
                    out[pl.ds(place, 1), :] = total
            return carry

        lax.fori_loop(0, count // group, some, 0)

    add_all(rec_row, rec_lane, rec_first, rec_second, (data_0, data_1))
    add_all(src_row, src_lane, src_first, src_second, (source_0, source_1))


def localize(cells, first, second, first_cell, shape):
    local = cells - first_cell
    valid = (local >= 0) & (local < shape[0] * shape[1] * shape[2])
    local = jnp.where(valid, local, 0)
    return (
        local // shape[2],
        local % shape[2],
        jnp.where(valid, first, 0.0),
        jnp.where(valid, second, 0.0),
    )


def injections(src, rec, first_cell, shape):
    flat = jax.ShapeDtypeStruct((shape[0] * shape[1], shape[2]), jnp.float32)
    outs = pl.pallas_call(
        scatter_kernel,
        out_shape=(flat,) * 4,
        in_specs=[pl.BlockSpec(memory_space=pltpu.SMEM)] * 8,
        out_specs=(pl.BlockSpec(memory_space=pltpu.VMEM),) * 4,
        compiler_params=pltpu.CompilerParams(vmem_limit_bytes=VMEM_GRANT),
        cost_estimate=pl.CostEstimate(flops=0, bytes_accessed=40 * 2**20, transcendentals=0),
        name="inject",
    )(*localize(*rec, first_cell, shape), *localize(*src, first_cell, shape))
    return [out.reshape(shape) for out in outs]


def load_fields(sources, fields, sems):
    step, blocks = pl.program_id(0), pl.num_programs(0)
    count = sources[0].shape[0] // REACH

    def copy(side, block):
        return pltpu.make_async_copy(
            sources[side].at[pl.ds(block * REACH, REACH)],
            fields[side].at[pl.ds((block + 1) * REACH, REACH)],
            sems.at[side, block],
        )

    @pl.when(step == 0)
    def _():
        for block in range(count):
            for side in range(2):
                copy(side, block).start()
        for field in fields:
            zero = jnp.zeros((REACH,) + field.shape[1:], jnp.float32)
            field[:REACH] = zero
            field[(count + 1) * REACH :] = zero
        for side in range(2):
            copy(side, 0).wait()

    @pl.when(step + 1 < blocks)
    def _():
        for side in range(2):
            copy(side, step + 1).wait()


def slab_laplace(place, fields, table_y, table_z):
    planes = [field[place] for field in fields]
    both = jnp.concatenate(planes, axis=1)
    high = both.astype(jnp.bfloat16)
    low = (both - high.astype(jnp.float32)).astype(jnp.bfloat16)
    total = jnp.dot(
        table_y[...], jnp.concatenate([high, low], axis=0), preferred_element_type=jnp.float32
    ) + jnp.dot(
        jnp.concatenate([high, low], axis=1), table_z[...], preferred_element_type=jnp.float32
    )
    width = fields[0].shape[2]
    laps = []
    for side, field in enumerate(fields):
        lap = total[:, side * width : (side + 1) * width] + MIDDLE * planes[side]
        for offset, weight in enumerate(WHOLE):
            lap += weight * (field[place + offset + 1] + field[place - offset - 1])
        laps.append(lap)
    return laps


def first_kernel(
    f_all, a_all, courant, f_old, a_late, source, data, table_y, table_z,
    accel, f_next, a_mid, f_now, a_now, sems,
):
    load_fields((f_all, a_all), (f_now, a_now), sems)
    for row in range(REACH):
        place = (pl.program_id(0) + 1) * REACH + row
        lap_f, lap_a = slab_laplace(place, (f_now, a_now), table_y, table_z)
        here = courant[row] * (1.0 / SCALE)
        accel_row = here * lap_f + source[row]
        accel[row] = accel_row
        f_next[row] = (2.0 * f_now[place] - f_old[row]) + accel_row
        a_mid[row] = (2.0 * a_now[place] - a_late[row]) + (here * lap_a + data[row])


def second_kernel(
    f_all, a_all, courant, a_old, accel, source, data, table_y, table_z, term,
    f_now, a_now, sems,
):
    load_fields((f_all, a_all), (f_now, a_now), sems)
    for row in range(REACH):
        place = (pl.program_id(0) + 1) * REACH + row
        lap_f, lap_a = slab_laplace(place, (f_now, a_now), table_y, table_z)
        here = courant[row] * (1.0 / SCALE)
        accel_second = here * lap_f + source[row]
        a_row = a_now[place]
        a_first = (2.0 * a_row - a_old[row]) + (here * lap_a + data[row])
        term[row] = a_first * accel[row] + a_row * accel_second


def slab_step(kernel, outs, field_f, field_a, others, tables):
    rows, width_y, width_z = field_f.shape
    blocks = rows // REACH
    here = pl.BlockSpec((REACH, width_y, width_z), lambda i: (i, 0, 0))
    whole = [pl.BlockSpec(table.shape, lambda i: (0, 0)) for table in tables]
    shape = jax.ShapeDtypeStruct(field_f.shape, jnp.float32)
    padded = pltpu.VMEM((rows + 2 * REACH, width_y, width_z), jnp.float32)
    return pl.pallas_call(
        kernel,
        grid=(blocks,),
        out_shape=(shape,) * outs,
        in_specs=[pl.BlockSpec(memory_space=pl.ANY)] * 2 + [here] * len(others) + whole,
        out_specs=(here,) * outs,
        scratch_shapes=[padded, padded, pltpu.SemaphoreType.DMA((2, blocks))],
        compiler_params=pltpu.CompilerParams(
            dimension_semantics=("arbitrary",), vmem_limit_bytes=VMEM_GRANT
        ),
        cost_estimate=pl.CostEstimate(
            flops=2**33, bytes_accessed=40 * 2**20, transcendentals=0
        ),
    )(field_f, field_a, *others, *tables)


def halo_terms(side, row, halo, field):
    total = None
    for offset, weight in enumerate(COEFS):
        reach = offset + 1
        plane = row - reach + REACH if side == 0 else row + reach - REACH
        if 0 <= plane < REACH:
            part = weight * halo[field, plane]
            total = part if total is None else total + part
    return total


def first_edge_kernel(
    halo_low, halo_high, courant, accel_in, next_in, mid_in, accel, f_next, a_mid, low, high
):
    for side, halo, edge in ((0, halo_low, low), (1, halo_high, high)):

        @pl.when(pl.program_id(0) == side)
        def _():
            for row in range(REACH):
                here = courant[row]
                add_f = here * halo_terms(side, row, halo, 0)
                add_a = here * halo_terms(side, row, halo, 1)
                accel[row] = accel_in[row] + add_f
                next_row = next_in[row] + add_f
                mid_row = mid_in[row] + add_a
                f_next[row] = next_row
                a_mid[row] = mid_row
                edge[0, row] = next_row
                edge[1, row] = mid_row


def second_edge_kernel(halo_low, halo_high, courant, accel, a_mid, term, edge):
    for side, halo in ((0, halo_low), (1, halo_high)):

        @pl.when(pl.program_id(0) == side)
        def _():
            for row in range(REACH):
                here = courant[row]
                add_f = here * halo_terms(side, row, halo, 0)
                add_a = here * halo_terms(side, row, halo, 1)
                edge[row] = term[row] + (add_a * accel[row] + a_mid[row] * add_f)


def edge_specs(shape):
    last = shape[0] // REACH - 1
    block = (REACH,) + shape[1:]
    both = pl.BlockSpec((2,) + block, lambda i: (0, 0, 0, 0))
    edge = pl.BlockSpec(block, lambda i: (i * last, 0, 0))
    side = pl.BlockSpec(block, lambda i: (i, 0, 0))
    return both, edge, side


EDGE_PARAMS = dict(dimension_semantics=("arbitrary",), vmem_limit_bytes=40 * 2**20)


def first_edges(low, high, courant, accel, f_next, a_mid):
    both, edge, _ = edge_specs(courant.shape)
    full = jax.ShapeDtypeStruct(courant.shape, jnp.float32)
    pair = jax.ShapeDtypeStruct(low.shape, jnp.float32)
    return pl.pallas_call(
        first_edge_kernel,
        grid=(2,),
        out_shape=(full, full, full, pair, pair),
        in_specs=[both, both, edge, edge, edge, edge],
        out_specs=(edge, edge, edge, both, both),
        input_output_aliases={3: 0, 4: 1, 5: 2},
        compiler_params=pltpu.CompilerParams(**EDGE_PARAMS),
        name="first_edges",
    )(low, high, courant, accel, f_next, a_mid)


def second_edges(low, high, courant, accel, a_mid, term):
    both, edge, side = edge_specs(courant.shape)
    shape = jax.ShapeDtypeStruct((2 * REACH,) + courant.shape[1:], jnp.float32)
    return pl.pallas_call(
        second_edge_kernel,
        grid=(2,),
        out_shape=shape,
        in_specs=[both, both, edge, edge, edge, edge],
        out_specs=side,
        compiler_params=pltpu.CompilerParams(**EDGE_PARAMS),
        name="second_edges",
    )(low, high, courant, accel, a_mid, term)


def pack_kernel(f_low, f_high, a_low, a_high, low, high):
    low[0], low[1] = f_low[...], a_low[...]
    high[0], high[1] = f_high[...], a_high[...]


def pack_edges(field_f, field_a):
    block = (REACH,) + field_f.shape[1:]
    last = field_f.shape[0] // REACH - 1
    low = pl.BlockSpec(block, lambda i: (0, 0, 0))
    high = pl.BlockSpec(block, lambda i: (last, 0, 0))
    both = pl.BlockSpec((2,) + block, lambda i: (0, 0, 0, 0))
    pair = jax.ShapeDtypeStruct((2,) + block, jnp.float32)
    return pl.pallas_call(
        pack_kernel,
        grid=(1,),
        out_shape=(pair, pair),
        in_specs=[low, high, low, high],
        out_specs=(both, both),
        compiler_params=pltpu.CompilerParams(vmem_limit_bytes=VMEM_GRANT),
        name="pack_edges",
    )(field_f, field_f, field_a, field_a)


def exchange(low_edge, high_edge):
    count = lax.axis_size("mp")
    upward = [(i, i + 1) for i in range(count - 1)]
    downward = [(i + 1, i) for i in range(count - 1)]
    from_low = lax.ppermute(high_edge, "mp", upward)
    from_high = lax.ppermute(low_edge, "mp", downward)
    return from_low, from_high


def sum_groups(term):
    count = lax.axis_size("shot")
    place = lax.axis_index("shot")
    rows, width_y, width_z = term.shape
    part = term.reshape(rows, count, width_y // count, width_z)
    bit = 1
    while bit < count:
        split = part.reshape(rows, part.shape[1] // 2, 2, part.shape[2], width_z)
        own = (place // bit) % 2
        mine = lax.dynamic_index_in_dim(split, own, 2, keepdims=False)
        other = lax.dynamic_index_in_dim(split, 1 - own, 2, keepdims=False)
        sent = lax.ppermute(other, "shot", [(i, i ^ bit) for i in range(count)])
        part = mine + sent
        bit *= 2
    return part[:, 0]


def slab_tables(table, count):
    rows = table.shape[0] // count
    local, sums, gains = [], [], []
    for me in range(count):
        own = slice(me * rows, (me + 1) * rows)
        local.append(table[own, own])
        sums.append(np.stack([table[me * rows, own], table[(me + 1) * rows - 1, own]]))
        gain = []
        for shift in range(1, count):
            source = (me - shift) % count
            seen = (source + 1) * rows - 1 if source < me else source * rows
            gain.append(table[own, seen] / table[seen, seen])
        gains.append(np.stack(gain, axis=1) if gain else np.zeros((rows, 0)))
    mix = np.concatenate([np.stack(local), np.stack(gains)], axis=2)
    return mix.astype(np.float32), np.stack(sums).astype(np.float32)


def mean_kernel(groups, inner, outer, sums, raw, planes):
    rows, edge = raw.shape[0], outer.shape[0] // 2
    total = [None, None]
    for row in range(rows):
        if row < edge:
            plane = outer[row]
        elif row < rows - edge:
            plane = inner[row - edge]
        else:
            plane = outer[row - rows + 2 * edge]
        plane = plane / groups
        raw[row] = plane
        for side in range(2):
            part = sums[side, row] * plane
            total[side] = part if row == 0 else total[side] + part
    planes[0], planes[1] = total


def make_smooth_kernel(count, group, lines):
    def kernel(raw, *refs):
        planes, (mix, table_z) = refs[: count - 1], refs[count - 1 : count + 1]
        pieces, mixed = refs[count + 1 : -1], refs[-1]
        rows = raw.shape[0]
        step = math.gcd(rows, 4)

        def some(index, carry):
            base = index * step
            sums = [None] * step
            for source in range(rows + count - 1):
                plane = raw[source] if source < rows else planes[source - rows][0]
                for extra in range(step):
                    part = mix[base + extra, source] * plane
                    sums[extra] = part if source == 0 else sums[extra] + part
            for extra in range(step):
                mixed[base + extra] = sums[extra]
            return carry

        lax.fori_loop(0, rows // step, some, 0)
        apart = rows // group
        for place in range(apart):
            stacked = jnp.concatenate(
                [mixed[part * apart + place] for part in range(group)], axis=0
            )
            turned = lax.dot_general(
                table_z[...],
                stacked,
                (((1,), (1,)), ((), ())),
                precision=HIGHEST,
                preferred_element_type=jnp.float32,
            )
            for target, piece in enumerate(pieces):
                piece[place] = turned[target * lines : (target + 1) * lines]

    return kernel


def make_last_kernel(count, group, groups):
    def kernel(*refs):
        pieces, table, out, spread = refs[:count], refs[count], refs[count + 1], refs[count + 2]
        apart, lines, lanes = pieces[0].shape
        width = out.shape[2]
        block = width // groups
        slab = lax.axis_index("mp")
        spread[...] = jnp.zeros(spread.shape, jnp.float32)
        for shift in range(count):
            number = lax.rem(slab + (count - shift), count)
            rows = table[pl.ds(pl.multiple_of(lax.rem(number, groups) * block, block), block), :]
            for part in range(group):
                column = (lax.div(number, groups) * group + part) * width
                top = shift * lanes + part * block
                spread[top : top + block, pl.ds(pl.multiple_of(column, width), width)] = rows
        whole = jnp.concatenate(
            [piece[...].reshape(apart * lines, lanes) for piece in pieces], axis=1
        )
        done = jnp.dot(whole, spread[...], precision=HIGHEST, preferred_element_type=jnp.float32)
        for place in range(count // groups * group):
            out[place * apart : (place + 1) * apart] = done[
                :, place * width : (place + 1) * width
            ].reshape(apart, lines, width)

    return kernel


VMEM = pl.BlockSpec(memory_space=pltpu.VMEM)
SMEM = pl.BlockSpec(memory_space=pltpu.SMEM)
GRANT = pltpu.CompilerParams(vmem_limit_bytes=40 * 2**20)


def smooth(inner, outer, slab_rows, width_y, width_z):
    slabs, groups = lax.axis_size("mp"), lax.axis_size("shot")
    slab, place = lax.axis_index("mp"), lax.axis_index("shot")
    ratio = slabs // groups
    lines_y, lines_z = width_y // groups, width_z // slabs
    group = max(1, 128 // lines_y)

    table_x, spread_x = smoothing_table(slab_rows * slabs, SMOOTH_X**2)
    table_y, spread_y = smoothing_table(width_y, SMOOTH_YZ**2)
    table_z, spread_z = smoothing_table(width_z, SMOOTH_YZ**2)
    table_y = table_y * (spread_x * spread_y * spread_z)
    mix, sums = (
        lax.dynamic_index_in_dim(jnp.asarray(table), slab, 0, keepdims=False)
        for table in slab_tables(table_x, slabs)
    )
    first = lax.rem(lax.rem(slab, ratio) * groups + place, slabs)
    table_z = jnp.asarray(np.concatenate([table_z, table_z]).astype(np.float32))
    table_z = lax.dynamic_slice_in_dim(table_z, first * lines_z, width_z, 0)
    table_y = jnp.asarray(table_y, jnp.float32)
    block = jax.ShapeDtypeStruct((slab_rows, lines_y, width_z), jnp.float32)
    raw, planes = pl.pallas_call(
        functools.partial(mean_kernel, float(groups)),
        out_shape=(block, jax.ShapeDtypeStruct((2, lines_y, width_z), jnp.float32)),
        in_specs=[VMEM, VMEM, SMEM],
        out_specs=(VMEM, VMEM),
        compiler_params=GRANT,
        name="mean",
    )(inner, outer, sums)
    received = []
    for shift in range(1, slabs):
        upward = jnp.where(slab + shift < slabs, 1, 0)
        sent = lax.dynamic_slice_in_dim(planes, upward, 1, 0)
        ring = [(i, (i + shift) % slabs) for i in range(slabs)]
        received.append(lax.ppermute(sent, "mp", ring))
    piece = jax.ShapeDtypeStruct((slab_rows // group, lines_z, group * lines_y), jnp.float32)
    pieces = pl.pallas_call(
        make_smooth_kernel(slabs, group, lines_z),
        out_shape=(piece,) * slabs,
        in_specs=[VMEM] * slabs + [SMEM, VMEM],
        out_specs=(VMEM,) * slabs,
        scratch_shapes=[pltpu.VMEM((slab_rows, lines_y, width_z), jnp.float32)],
        compiler_params=GRANT,
        name="smooth_xz",
    )(raw, *received, mix, table_z)
    arrived = []
    for shift, sent in enumerate(pieces):
        pairs = []
        for m in range(slabs):
            for s in range(groups):
                target = ((m % ratio) * groups + s + shift) % slabs
                pairs.append((m * groups + s, target * groups + m // ratio))
        arrived.append(lax.ppermute(sent, ("mp", "shot"), pairs))
    done = pl.pallas_call(
        make_last_kernel(slabs, group, groups),
        out_shape=jax.ShapeDtypeStruct((slab_rows * ratio, lines_z, width_y), jnp.float32),
        in_specs=[VMEM] * (slabs + 1),
        out_specs=VMEM,
        scratch_shapes=[
            pltpu.VMEM((slabs * group * lines_y, ratio * group * width_y), jnp.float32)
        ],
        compiler_params=GRANT,
        name="smooth_y",
    )(*arrived, table_y)
    return raw, jnp.swapaxes(done, 1, 2)


def one_device(
    courant,
    forward_old,
    forward_now,
    adjoint_late,
    adjoint_now,
    src_cell,
    src_sign,
    wavelet,
    rec_cell,
    rec_data,
):
    shape = courant.shape
    slab_rows = shape[0]
    first_row = lax.axis_index("mp") * slab_rows
    old_fwd, now_fwd = forward_old[0], forward_now[0]
    late_adj, now_adj = adjoint_late[0], adjoint_now[0]
    tables = stencil_tables(shape[1], shape[2])

    signed = (2 * src_sign[0] - 1).astype(jnp.float32)
    halo_low, halo_high = exchange(*pack_edges(now_fwd, now_adj))
    first_cell = first_row * shape[1] * shape[2]
    source_0, source_1, data_0, data_1 = injections(
        (src_cell[0], signed * wavelet[0, 0], signed * wavelet[0, 1]),
        (rec_cell, rec_data[0, 0], rec_data[0, 1]),
        first_cell,
        shape,
    )
    accel, next_fwd, mid_adj = slab_step(
        first_kernel, 3, now_fwd, now_adj,
        (courant, old_fwd, late_adj, source_0, data_0), tables,
    )
    accel, next_fwd, mid_adj, low_edge, high_edge = first_edges(
        halo_low, halo_high, courant, accel, next_fwd, mid_adj
    )
    halo_low, halo_high = exchange(low_edge, high_edge)
    (term,) = slab_step(
        second_kernel, 1, next_fwd, mid_adj,
        (courant, now_adj, accel, source_1, data_1), tables,
    )
    inner = sum_groups(term[REACH:-REACH])
    edges = second_edges(halo_low, halo_high, courant, accel, mid_adj, term)
    outer = sum_groups(edges)
    return smooth(inner, outer, shape[0], shape[1], shape[2])


def solution(mesh):
    return jax.shard_map(
        one_device,
        mesh=mesh,
        in_specs=(
            P(("parts", "mp"), None, None),
            P(("parts", "shot"), "mp", None, None),
            P(("parts", "shot"), "mp", None, None),
            P(("parts", "shot"), "mp", None, None),
            P(("parts", "shot"), "mp", None, None),
            P(("parts", "shot"), None),
            P(("parts", "shot"), None),
            P(("parts", "shot"), None, None),
            P("parts"),
            P(("parts", "shot"), None, None),
        ),
        out_specs=(P(("parts", "mp"), "shot", None), P(("parts", "shot"), None, "mp")),
        check_vma=False,
    )
```

```python
import functools
import math

import jax
import jax.numpy as jnp
import numpy as np
from jax import lax
from jax.experimental import pallas as pl
from jax.experimental.pallas import tpu as pltpu
from jax.sharding import PartitionSpec as P

SMOOTH_X = 32
SMOOTH_YZ = 4
COEFS = (8.0 / 5.0, -1.0 / 5.0, 8.0 / 315.0, -1.0 / 560.0)
CENTER = -205.0 / 72.0
REACH = 4
HIGHEST = lax.Precision.HIGHEST

VMEM_GRANT = 60 * 2**20


def smoothing_table(length, strength):
    counter = np.arange(1, length + 1, dtype=np.float64)
    sines = np.sin(np.pi * np.outer(counter, counter) / (length + 1))
    half_sine = np.sin(np.pi * counter / (2 * (length + 1)))
    resp = 1.0 / (1.0 + strength * 4.0 * half_sine**2)
    table = 2.0 / (length + 1) * (sines * resp[None, :]) @ sines
    return table, 1.0 / math.sqrt(np.mean(resp * resp))


SCALE = 5040.0
WHOLE = tuple(float(round(SCALE * weight)) for weight in COEFS)
MIDDLE = 3.0 * float(round(SCALE * CENTER))


def stencil_tables(width_y, width_z):
    def bands(length):
        return sum(
            weight * (np.eye(length, k=offset + 1) + np.eye(length, k=-offset - 1))
            for offset, weight in enumerate(WHOLE)
        )

    band_y = bands(width_y)
    band_z = np.kron(np.eye(2), bands(width_z))
    return (
        jnp.asarray(np.concatenate([band_y, band_y], axis=1), jnp.bfloat16),
        jnp.asarray(np.concatenate([band_z, band_z], axis=0), jnp.bfloat16),
    )


def inject(rows, columns, values, out):
    out[...] = jnp.zeros(out.shape, jnp.float32)
    lanes = lax.broadcasted_iota(jnp.int32, (1, out.shape[1]), 1)
    count = rows.shape[0]
    group = math.gcd(count, 8)

    def some(step, carry):
        items = [step * group + extra for extra in range(group)]
        places = [rows[item] for item in items]
        added = [jnp.where(lanes == columns[item], values[item], 0.0) for item in items]
        sums = []
        for late in range(group):
            total = added[late]
            for early in range(late):
                total += jnp.where(places[early] == places[late], added[early], 0.0)
            sums.append(out[pl.ds(places[late], 1), :] + total)
        for place, total in zip(places, sums):
            out[pl.ds(place, 1), :] = total
        return carry

    lax.fori_loop(0, count // group, some, 0)


def localize(cells, first, second, first_cell, shape):
    local = cells - first_cell
    valid = (local >= 0) & (local < shape[0] * shape[1] * shape[2])
    local = jnp.where(valid, local, 0)
    return (
        local // shape[2],
        local % shape[2],
        jnp.where(valid, first, 0.0),
        jnp.where(valid, second, 0.0),
    )


def load_fields(sources, fields, sems, src, rec):
    step, blocks = pl.program_id(0), pl.num_programs(0)
    count = sources[0].shape[0] // REACH

    def copy(side, block):
        return pltpu.make_async_copy(
            sources[side].at[pl.ds(block * REACH, REACH)],
            fields[side].at[pl.ds((block + 1) * REACH, REACH)],
            sems.at[side, block],
        )

    @pl.when(step == 0)
    def _():
        for block in range(count):
            for side in range(2):
                copy(side, block).start()
        for field in fields:
            zero = jnp.zeros((REACH,) + field.shape[1:], jnp.float32)
            field[:REACH] = zero
            field[(count + 1) * REACH :] = zero
        inject(*src)
        inject(*rec)
        for side in range(2):
            copy(side, 0).wait()

    @pl.when(step + 1 < blocks)
    def _():
        for side in range(2):
            copy(side, step + 1).wait()


def slab_laplace(place, fields, table_y, table_z):
    planes = [field[place] for field in fields]
    both = jnp.concatenate(planes, axis=1)
    high = both.astype(jnp.bfloat16)
    low = (both - high.astype(jnp.float32)).astype(jnp.bfloat16)
    total = jnp.dot(
        table_y[...], jnp.concatenate([high, low], axis=0), preferred_element_type=jnp.float32
    ) + jnp.dot(
        jnp.concatenate([high, low], axis=1), table_z[...], preferred_element_type=jnp.float32
    )
    width = fields[0].shape[2]
    laps = []
    for side, field in enumerate(fields):
        lap = total[:, side * width : (side + 1) * width] + MIDDLE * planes[side]
        for offset, weight in enumerate(WHOLE):
            lap += weight * (field[place + offset + 1] + field[place - offset - 1])
        laps.append(lap)
    return laps


def plane_of(flat, place, block):
    width = block.shape[1]
    return flat[pl.ds(pl.multiple_of((place - REACH) * width, width), width), :]


def first_kernel(
    f_all, a_all, courant, f_old, a_late, table_y, table_z,
    src_row, src_lane, src_value, rec_row, rec_lane, rec_value,
    accel, f_next, a_mid, f_now, a_now, source, data, sems,
):
    load_fields(
        (f_all, a_all), (f_now, a_now), sems,
        (src_row, src_lane, src_value, source), (rec_row, rec_lane, rec_value, data),
    )
    for row in range(REACH):
        place = (pl.program_id(0) + 1) * REACH + row
        lap_f, lap_a = slab_laplace(place, (f_now, a_now), table_y, table_z)
        here = courant[row] * (1.0 / SCALE)
        accel_row = here * lap_f + plane_of(source, place, courant)
        accel[row] = accel_row
        f_next[row] = (2.0 * f_now[place] - f_old[row]) + accel_row
        a_mid[row] = (2.0 * a_now[place] - a_late[row]) + (here * lap_a + plane_of(data, place, courant))


def second_kernel(
    f_all, a_all, courant, a_old, accel, table_y, table_z,
    src_row, src_lane, src_value, rec_row, rec_lane, rec_value,
    term, f_now, a_now, source, data, sems,
):
    load_fields(
        (f_all, a_all), (f_now, a_now), sems,
        (src_row, src_lane, src_value, source), (rec_row, rec_lane, rec_value, data),
    )
    for row in range(REACH):
        place = (pl.program_id(0) + 1) * REACH + row
        lap_f, lap_a = slab_laplace(place, (f_now, a_now), table_y, table_z)
        here = courant[row] * (1.0 / SCALE)
        accel_second = here * lap_f + plane_of(source, place, courant)
        a_row = a_now[place]
        a_first = (2.0 * a_row - a_old[row]) + (here * lap_a + plane_of(data, place, courant))
        term[row] = a_first * accel[row] + a_row * accel_second


def slab_step(kernel, outs, field_f, field_a, others, tables, lists):
    rows, width_y, width_z = field_f.shape
    blocks = rows // REACH
    here = pl.BlockSpec((REACH, width_y, width_z), lambda i: (i, 0, 0))
    whole = [pl.BlockSpec(table.shape, lambda i: (0, 0)) for table in tables]
    shape = jax.ShapeDtypeStruct(field_f.shape, jnp.float32)
    flat = pltpu.VMEM((rows * width_y, width_z), jnp.float32)
    padded = pltpu.VMEM((rows + 2 * REACH, width_y, width_z), jnp.float32)
    return pl.pallas_call(
        kernel,
        grid=(blocks,),
        out_shape=(shape,) * outs,
        in_specs=[pl.BlockSpec(memory_space=pl.ANY)] * 2 + [here] * len(others) + whole + [SMEM] * 6,
        out_specs=(here,) * outs,
        scratch_shapes=[padded, padded, flat, flat, pltpu.SemaphoreType.DMA((2, blocks))],
        compiler_params=pltpu.CompilerParams(
            dimension_semantics=("arbitrary",), vmem_limit_bytes=VMEM_GRANT
        ),
        cost_estimate=pl.CostEstimate(
            flops=2**33, bytes_accessed=40 * 2**20, transcendentals=0
        ),
    )(field_f, field_a, *others, *tables, *lists)


def halo_terms(side, row, halo, field):
    total = None
    for offset, weight in enumerate(COEFS):
        reach = offset + 1
        plane = row - reach + REACH if side == 0 else row + reach - REACH
        if 0 <= plane < REACH:
            part = weight * halo[field, plane]
            total = part if total is None else total + part
    return total


def first_edge_kernel(
    halo_low, halo_high, courant, accel_in, next_in, mid_in, accel, f_next, a_mid, low, high
):
    for side, halo, edge in ((0, halo_low, low), (1, halo_high, high)):

        @pl.when(pl.program_id(0) == side)
        def _():
            for row in range(REACH):
                here = courant[row]
                add_f = here * halo_terms(side, row, halo, 0)
                add_a = here * halo_terms(side, row, halo, 1)
                accel[row] = accel_in[row] + add_f
                next_row = next_in[row] + add_f
                mid_row = mid_in[row] + add_a
                f_next[row] = next_row
                a_mid[row] = mid_row
                edge[0, row] = next_row
                edge[1, row] = mid_row


def second_edge_kernel(halo_low, halo_high, courant, accel, a_mid, term, edge):
    for side, halo in ((0, halo_low), (1, halo_high)):

        @pl.when(pl.program_id(0) == side)
        def _():
            for row in range(REACH):
                here = courant[row]
                add_f = here * halo_terms(side, row, halo, 0)
                add_a = here * halo_terms(side, row, halo, 1)
                edge[row] = term[row] + (add_a * accel[row] + a_mid[row] * add_f)


def edge_specs(shape):
    last = shape[0] // REACH - 1
    block = (REACH,) + shape[1:]
    both = pl.BlockSpec((2,) + block, lambda i: (0, 0, 0, 0))
    edge = pl.BlockSpec(block, lambda i: (i * last, 0, 0))
    side = pl.BlockSpec(block, lambda i: (i, 0, 0))
    return both, edge, side


EDGE_PARAMS = dict(dimension_semantics=("arbitrary",), vmem_limit_bytes=VMEM_GRANT)


def first_edges(low, high, courant, accel, f_next, a_mid):
    both, edge, _ = edge_specs(courant.shape)
    full = jax.ShapeDtypeStruct(courant.shape, jnp.float32)
    pair = jax.ShapeDtypeStruct(low.shape, jnp.float32)
    return pl.pallas_call(
        first_edge_kernel,
        grid=(2,),
        out_shape=(full, full, full, pair, pair),
        in_specs=[both, both, edge, edge, edge, edge],
        out_specs=(edge, edge, edge, both, both),
        input_output_aliases={3: 0, 4: 1, 5: 2},
        compiler_params=pltpu.CompilerParams(**EDGE_PARAMS),
        name="first_edges",
    )(low, high, courant, accel, f_next, a_mid)


def second_edges(low, high, courant, accel, a_mid, term):
    both, edge, side = edge_specs(courant.shape)
    shape = jax.ShapeDtypeStruct((2 * REACH,) + courant.shape[1:], jnp.float32)
    return pl.pallas_call(
        second_edge_kernel,
        grid=(2,),
        out_shape=shape,
        in_specs=[both, both, edge, edge, edge, edge],
        out_specs=side,
        compiler_params=pltpu.CompilerParams(**EDGE_PARAMS),
        name="second_edges",
    )(low, high, courant, accel, a_mid, term)


def pack_kernel(f_low, f_high, a_low, a_high, low, high):
    low[0], low[1] = f_low[...], a_low[...]
    high[0], high[1] = f_high[...], a_high[...]


def pack_edges(field_f, field_a):
    block = (REACH,) + field_f.shape[1:]
    last = field_f.shape[0] // REACH - 1
    low = pl.BlockSpec(block, lambda i: (0, 0, 0))
    high = pl.BlockSpec(block, lambda i: (last, 0, 0))
    both = pl.BlockSpec((2,) + block, lambda i: (0, 0, 0, 0))
    pair = jax.ShapeDtypeStruct((2,) + block, jnp.float32)
    return pl.pallas_call(
        pack_kernel,
        grid=(1,),
        out_shape=(pair, pair),
        in_specs=[low, high, low, high],
        out_specs=(both, both),
        compiler_params=pltpu.CompilerParams(vmem_limit_bytes=VMEM_GRANT),
        name="pack_edges",
    )(field_f, field_f, field_a, field_a)


def exchange(low_edge, high_edge):
    count = lax.axis_size("mp")
    upward = [(i, i + 1) for i in range(count - 1)]
    downward = [(i + 1, i) for i in range(count - 1)]
    from_low = lax.ppermute(high_edge, "mp", upward)
    from_high = lax.ppermute(low_edge, "mp", downward)
    return from_low, from_high


def sum_groups(term):
    count = lax.axis_size("shot")
    place = lax.axis_index("shot")
    rows, width_y, width_z = term.shape
    part = term.reshape(rows, count, width_y // count, width_z)
    bit = 1
    while bit < count:
        split = part.reshape(rows, part.shape[1] // 2, 2, part.shape[2], width_z)
        own = (place // bit) % 2
        mine = lax.dynamic_index_in_dim(split, own, 2, keepdims=False)
        other = lax.dynamic_index_in_dim(split, 1 - own, 2, keepdims=False)
        sent = lax.ppermute(other, "shot", [(i, i ^ bit) for i in range(count)])
        part = mine + sent
        bit *= 2
    return part[:, 0]


def slab_tables(table, count):
    rows = table.shape[0] // count
    local, sums, gains = [], [], []
    for me in range(count):
        own = slice(me * rows, (me + 1) * rows)
        local.append(table[own, own])
        sums.append(np.stack([table[me * rows, own], table[(me + 1) * rows - 1, own]]))
        gain = []
        for shift in range(1, count):
            source = (me - shift) % count
            seen = (source + 1) * rows - 1 if source < me else source * rows
            gain.append(table[own, seen] / table[seen, seen])
        gains.append(np.stack(gain, axis=1) if gain else np.zeros((rows, 0)))
    mix = np.concatenate([np.stack(local), np.stack(gains)], axis=2)
    return mix.astype(np.float32), np.stack(sums).astype(np.float32)


def mean_kernel(groups, inner, outer, sums, raw, planes):
    rows, edge = raw.shape[0], outer.shape[0] // 2
    total = [None, None]
    for row in range(rows):
        if row < edge:
            plane = outer[row]
        elif row < rows - edge:
            plane = inner[row - edge]
        else:
            plane = outer[row - rows + 2 * edge]
        plane = plane / groups
        raw[row] = plane
        for side in range(2):
            part = sums[side, row] * plane
            total[side] = part if row == 0 else total[side] + part
    planes[0], planes[1] = total


def make_smooth_kernel(count, group, lines):
    def kernel(raw, *refs):
        planes, (mix, table_z) = refs[: count - 1], refs[count - 1 : count + 1]
        pieces, mixed = refs[count + 1 : -1], refs[-1]
        rows = raw.shape[0]
        step = math.gcd(rows, 4)

        def some(index, carry):
            base = index * step
            sums = [None] * step
            for source in range(rows + count - 1):
                plane = raw[source] if source < rows else planes[source - rows][0]
                for extra in range(step):
                    part = mix[base + extra, source] * plane
                    sums[extra] = part if source == 0 else sums[extra] + part
            for extra in range(step):
                mixed[base + extra] = sums[extra]
            return carry

        lax.fori_loop(0, rows // step, some, 0)
        apart = rows // group
        for place in range(apart):
            stacked = jnp.concatenate(
                [mixed[part * apart + place] for part in range(group)], axis=0
            )
            turned = lax.dot_general(
                table_z[...],
                stacked,
                (((1,), (1,)), ((), ())),
                precision=HIGHEST,
                preferred_element_type=jnp.float32,
            )
            for target, piece in enumerate(pieces):
                piece[place] = turned[target * lines : (target + 1) * lines]

    return kernel


def make_last_kernel(count, group, groups):
    def kernel(*refs):
        pieces, table, out, spread = refs[:count], refs[count], refs[count + 1], refs[count + 2]
        apart, lines, lanes = pieces[0].shape
        width = out.shape[2]
        block = width // groups
        slab = lax.axis_index("mp")
        spread[...] = jnp.zeros(spread.shape, jnp.float32)
        for shift in range(count):
            number = lax.rem(slab + (count - shift), count)
            rows = table[pl.ds(pl.multiple_of(lax.rem(number, groups) * block, block), block), :]
            for part in range(group):
                column = (lax.div(number, groups) * group + part) * width
                top = shift * lanes + part * block
                spread[top : top + block, pl.ds(pl.multiple_of(column, width), width)] = rows
        whole = jnp.concatenate(
            [piece[...].reshape(apart * lines, lanes) for piece in pieces], axis=1
        )
        done = jnp.dot(whole, spread[...], precision=HIGHEST, preferred_element_type=jnp.float32)
        for place in range(count // groups * group):
            out[place * apart : (place + 1) * apart] = done[
                :, place * width : (place + 1) * width
            ].reshape(apart, lines, width)

    return kernel


VMEM = pl.BlockSpec(memory_space=pltpu.VMEM)
SMEM = pl.BlockSpec(memory_space=pltpu.SMEM)
GRANT = pltpu.CompilerParams(vmem_limit_bytes=40 * 2**20)


def smooth(inner, outer, slab_rows, width_y, width_z):
    slabs, groups = lax.axis_size("mp"), lax.axis_size("shot")
    slab, place = lax.axis_index("mp"), lax.axis_index("shot")
    ratio = slabs // groups
    lines_y, lines_z = width_y // groups, width_z // slabs
    group = max(1, 128 // lines_y)

    table_x, spread_x = smoothing_table(slab_rows * slabs, SMOOTH_X**2)
    table_y, spread_y = smoothing_table(width_y, SMOOTH_YZ**2)
    table_z, spread_z = smoothing_table(width_z, SMOOTH_YZ**2)
    table_y = table_y * (spread_x * spread_y * spread_z)
    mix, sums = (
        lax.dynamic_index_in_dim(jnp.asarray(table), slab, 0, keepdims=False)
        for table in slab_tables(table_x, slabs)
    )
    first = lax.rem(lax.rem(slab, ratio) * groups + place, slabs)
    table_z = jnp.asarray(np.concatenate([table_z, table_z]).astype(np.float32))
    table_z = lax.dynamic_slice_in_dim(table_z, first * lines_z, width_z, 0)
    table_y = jnp.asarray(table_y, jnp.float32)
    block = jax.ShapeDtypeStruct((slab_rows, lines_y, width_z), jnp.float32)
    raw, planes = pl.pallas_call(
        functools.partial(mean_kernel, float(groups)),
        out_shape=(block, jax.ShapeDtypeStruct((2, lines_y, width_z), jnp.float32)),
        in_specs=[VMEM, VMEM, SMEM],
        out_specs=(VMEM, VMEM),
        compiler_params=GRANT,
        name="mean",
    )(inner, outer, sums)
    received = []
    for shift in range(1, slabs):
        upward = jnp.where(slab + shift < slabs, 1, 0)
        sent = lax.dynamic_slice_in_dim(planes, upward, 1, 0)
        ring = [(i, (i + shift) % slabs) for i in range(slabs)]
        received.append(lax.ppermute(sent, "mp", ring))
    piece = jax.ShapeDtypeStruct((slab_rows // group, lines_z, group * lines_y), jnp.float32)
    pieces = pl.pallas_call(
        make_smooth_kernel(slabs, group, lines_z),
        out_shape=(piece,) * slabs,
        in_specs=[VMEM] * slabs + [SMEM, VMEM],
        out_specs=(VMEM,) * slabs,
        scratch_shapes=[pltpu.VMEM((slab_rows, lines_y, width_z), jnp.float32)],
        compiler_params=GRANT,
        name="smooth_xz",
    )(raw, *received, mix, table_z)
    arrived = []
    for shift, sent in enumerate(pieces):
        pairs = []
        for m in range(slabs):
            for s in range(groups):
                target = ((m % ratio) * groups + s + shift) % slabs
                pairs.append((m * groups + s, target * groups + m // ratio))
        arrived.append(lax.ppermute(sent, ("mp", "shot"), pairs))
    done = pl.pallas_call(
        make_last_kernel(slabs, group, groups),
        out_shape=jax.ShapeDtypeStruct((slab_rows * ratio, lines_z, width_y), jnp.float32),
        in_specs=[VMEM] * (slabs + 1),
        out_specs=VMEM,
        scratch_shapes=[
            pltpu.VMEM((slabs * group * lines_y, ratio * group * width_y), jnp.float32)
        ],
        compiler_params=GRANT,
        name="smooth_y",
    )(*arrived, table_y)
    return raw, jnp.swapaxes(done, 1, 2)


def one_device(
    courant,
    forward_old,
    forward_now,
    adjoint_late,
    adjoint_now,
    src_cell,
    src_sign,
    wavelet,
    rec_cell,
    rec_data,
):
    shape = courant.shape
    slab_rows = shape[0]
    first_row = lax.axis_index("mp") * slab_rows
    old_fwd, now_fwd = forward_old[0], forward_now[0]
    late_adj, now_adj = adjoint_late[0], adjoint_now[0]
    tables = stencil_tables(shape[1], shape[2])

    signed = (2 * src_sign[0] - 1).astype(jnp.float32)
    halo_low, halo_high = exchange(*pack_edges(now_fwd, now_adj))
    first_cell = first_row * shape[1] * shape[2]
    src = localize(
        src_cell[0], signed * wavelet[0, 0], signed * wavelet[0, 1], first_cell, shape
    )
    rec = localize(rec_cell, rec_data[0, 0], rec_data[0, 1], first_cell, shape)
    lists = [(*src[:2], src[step], *rec[:2], rec[step]) for step in (2, 3)]
    accel, next_fwd, mid_adj = slab_step(
        first_kernel, 3, now_fwd, now_adj,
        (courant, old_fwd, late_adj), tables, lists[0],
    )
    accel, next_fwd, mid_adj, low_edge, high_edge = first_edges(
        halo_low, halo_high, courant, accel, next_fwd, mid_adj
    )
    halo_low, halo_high = exchange(low_edge, high_edge)
    (term,) = slab_step(
        second_kernel, 1, next_fwd, mid_adj,
        (courant, now_adj, accel), tables, lists[1],
    )
    inner = sum_groups(term[REACH:-REACH])
    edges = second_edges(halo_low, halo_high, courant, accel, mid_adj, term)
    outer = sum_groups(edges)
    return smooth(inner, outer, shape[0], shape[1], shape[2])


def solution(mesh):
    return jax.shard_map(
        one_device,
        mesh=mesh,
        in_specs=(
            P(("parts", "mp"), None, None),
            P(("parts", "shot"), "mp", None, None),
            P(("parts", "shot"), "mp", None, None),
            P(("parts", "shot"), "mp", None, None),
            P(("parts", "shot"), "mp", None, None),
            P(("parts", "shot"), None),
            P(("parts", "shot"), None),
            P(("parts", "shot"), None, None),
            P("parts"),
            P(("parts", "shot"), None, None),
        ),
        out_specs=(P(("parts", "mp"), "shot", None), P(("parts", "shot"), None, "mp")),
        check_vma=False,
    )
```
